32 devices in a mesh: pipe: 4 (over x, core), fsdp: 8 (over z, y).
Axes of the slice: x: 2, y: 2, z: 4, core: 2. Of those that a mesh axis runs over, the one named last changes fastest.
Arguments:
- saved: bfloat16 [4, 8, 3, 64, 4096], P('pipe', 'fsdp'), may hold values from -6 to 6
- cot_in: bfloat16 [4, 8, 64, 4096], P('pipe', 'fsdp'), may hold values from -6 to 6
- weights: bfloat16 [2, 4, 4096, 1024], P(None, 'pipe', 'fsdp'), may hold values from -0.09375 to 0.09375
- gains: bfloat16 [2, 4, 4096], P(None, 'pipe', 'fsdp'), may hold values from 0.099609375 to 1.8984375
- lengths: int32 [4, 8], P(None, 'fsdp'), may hold values from 1 to 64, 384 in all within a row
- segments: int32 [4, 8, 64], P(None, 'fsdp'), may hold values from 0 to 3, never falling along the last dimension, each value on 1 to 32 neighbouring positions
Outputs:
- cot_out: bfloat16 [4, 8, 64, 4096], P('pipe', 'fsdp')
- grad_kv: bfloat16 [2, 4, 4096, 1024], P(None, 'pipe', 'fsdp')
- grad_gain: bfloat16 [2, 4, 4096], P(None, 'pipe', 'fsdp')
The draws below stay inside these ranges and needn't reach their ends.
Inputs may be any that keep to these rules, and one draw needn't show every extreme that they name: The lengths of the 8 micro-batches of one j sum to 384 and the largest is 64. `segments`: document numbers never fall along the slots; a document spans at most 32 slots.
All inputs are finite; a program needn't handle non-finite values. No bound on the sum of `lengths` on one device may be relied on, other than what follows from the above.
Results may differ from the reference program's by a relative error of at most 0.02.
Values may be sent and summed in bfloat16 or wider, within the bound.
A program may use at most 128 MiB of HBM per device.

```python
import math
import jax
import jax.numpy as jnp
import numpy as np
from jax import lax

D = 4096
HEAD_SIZE = 128
KEY_VALUE_HEADS = 4
S = 64
TICKS = 3
KVW = 1024
N_PIPE = 4
N_FSDP = 8


def block_scale(rng, shape, cuts, least, largest):
    def one(axis_at, blocks):
        draws = jax.random.uniform(jax.random.fold_in(jax.random.fold_in(rng, 6), axis_at), (blocks,), jnp.float32, least / len(cuts), largest / len(cuts))
        return jnp.repeat(jnp.exp(draws), shape[axis_at] // blocks).reshape((-1,) + (1,) * (len(shape) - axis_at - 1))

    level = one(*cuts[0])
    for cut in cuts[1:]:
        level = level * one(*cut)
    return level


def length_profile(amount, total, reach, lean):
    loads = [(1 << 20) // math.isqrt(standing ** lean) + 1 for standing in range(2, amount + 1)]
    spare, holding = total - reach - (amount - 1), [1] * (amount - 1)
    while spare > 0:
        free = [i for i in range(amount - 1) if holding[i] < reach]
        mass, remaining = sum([loads[i] for i in free]), spare
        for i in free:
            more = min(reach - holding[i], max(1, remaining * loads[i] // mass), spare)
            holding[i] = holding[i] + more
            spare = spare - more
    return np.array([reach] + holding)


def ragged(stream_key, count, total, limit, skew):
    if count == 2:
        one = jax.random.randint(stream_key, (), max(1, total - limit), min(limit, total - 1) + 1)
        return jnp.stack([one, total - one])
    tallies = jnp.asarray(length_profile(count, total, limit, skew), jnp.int32)
    pairs = (count - 1) // 2
    donor, sink = tallies[1:1 + 2 * pairs:2], tallies[2:2 + 2 * pairs:2]
    room = jnp.minimum(donor - 1, limit - sink)
    moved = jax.random.randint(jax.random.fold_in(stream_key, 1), (pairs,), 0, 1 << 20) % (room + 1)
    tallies = tallies.at[1:1 + 2 * pairs:2].set(donor - moved).at[2:2 + 2 * pairs:2].set(sink + moved)
    return tallies[jax.random.permutation(jax.random.fold_in(stream_key, 2), count)]


def normal_values(stream_key, dims, deviation, limit, pieces=(), kind=jnp.bfloat16):
    result = deviation * jax.random.normal(stream_key, dims, jnp.float32)
    if pieces:
        result = result * block_scale(stream_key, dims, pieces, -0.22, 0.18)
    return jnp.clip(result, -limit, limit).astype(kind)


def setup_inputs(seed: int = 0) -> dict:
    key_list = jax.random.split(jax.random.key(seed), 7)
    return {
        "saved": normal_values(key_list[0], (N_PIPE, N_FSDP, TICKS, S, D), 1.0, 6.0, ((0, 4), (1, 8))),
        "cot_in": normal_values(key_list[1], (N_PIPE, N_FSDP, S, D), 1.0, 6.0, ((0, 4), (1, 8))),
        "weights": normal_values(key_list[2], (2, N_PIPE, D, KVW), D ** -0.5, 0.09375, ((1, 4), (2, 8))),
        "gains": jnp.clip(1.0 + 0.18 * jax.random.normal(key_list[3], (2, N_PIPE, D), jnp.float32), 0.099609375, 1.8984375).astype(jnp.bfloat16),
        "lengths": jax.vmap(lambda own: ragged(own, N_FSDP, 3 * N_FSDP * S // 4, S, 2))(jax.random.split(key_list[4], N_PIPE)).reshape((N_PIPE, N_FSDP)).astype(jnp.int32),
        "segments": jax.vmap(lambda own: jnp.searchsorted(jnp.cumsum(ragged(own, 4, S, S // 2, 1)), jnp.arange(S), side="right"))(jax.random.split(key_list[5], N_PIPE * N_FSDP)).reshape((N_PIPE, N_FSDP, S)).astype(jnp.int32),
    }


EPS = 1e-05

def normalize(resid, gain):
    factor = lax.rsqrt(lax.optimization_barrier(jnp.mean(resid * resid, axis=-1, keepdims=True)) + EPS)
    return resid * factor * gain

def attend(resid, normalized_input, key_value_pair, length, segment):
    item_count = resid.shape[0]
    model_width = resid.shape[1]
    query_groups = model_width // HEAD_SIZE // KEY_VALUE_HEADS
    query_rows = normalized_input.astype(jnp.bfloat16).reshape(item_count, KEY_VALUE_HEADS, query_groups, HEAD_SIZE)
    key_rows = key_value_pair[:, :KEY_VALUE_HEADS * HEAD_SIZE].astype(jnp.bfloat16).reshape(item_count, KEY_VALUE_HEADS, HEAD_SIZE)
    value_rows = key_value_pair[:, KEY_VALUE_HEADS * HEAD_SIZE:].astype(jnp.bfloat16).reshape(item_count, KEY_VALUE_HEADS, HEAD_SIZE)
    scores = jnp.einsum('pkgd,qkd->kgpq', query_rows, key_rows, preferred_element_type=jnp.float32) * HEAD_SIZE ** (-0.5)
    place = jnp.arange(item_count, dtype=jnp.int32)
    allowed = (segment[:, None] == segment[None, :]) & (place[None, :] <= place[:, None]) & (place[None, :] < length)
    allowed = allowed | (place[:, None] == place[None, :])
    scores = jnp.where(allowed, scores, -1e+30)
    peak = lax.optimization_barrier(jnp.max(scores, axis=-1, keepdims=True))
    expo = jnp.exp(scores - peak)
    probs = (expo / lax.optimization_barrier(jnp.sum(expo, axis=-1, keepdims=True))).astype(jnp.bfloat16)
    mixed = jnp.einsum('kgpq,qkd->pkgd', probs, value_rows, preferred_element_type=jnp.float32).reshape(item_count, model_width)
    valid = (place < length).astype(jnp.float32)
    return resid + mixed * valid[:, None]

def attend_back(resid, normalized_input, key_value_pair, cotangent, length, segment):

    def inner(first, second, third):
        return attend(first, second, third, length, segment)
    _, pull = jax.vjp(inner, resid, normalized_input, key_value_pair)
    direct, normed_cot, keyval_cot = pull(cotangent.astype(jnp.float32))
    return (direct, normed_cot, keyval_cot.astype(jnp.bfloat16))

def layer_back(saved_in, cotangent, gain, weight, length, segment):
    resid = saved_in.astype(jnp.float32)
    normalized_input, front_pull = jax.vjp(normalize, resid, gain.astype(jnp.float32))
    normed_b = normalized_input.astype(jnp.bfloat16)
    key_value_pair = jnp.dot(normed_b, weight, preferred_element_type=jnp.float32)
    direct, normed_cot, keyval_cot = attend_back(resid, normalized_input, key_value_pair, cotangent, length, segment)
    normed_total = normed_cot + jnp.dot(keyval_cot, weight.T, preferred_element_type=jnp.float32)
    resid_cot, gain_cot = front_pull(normed_total)
    fresh = (direct + resid_cot).astype(jnp.bfloat16)
    return (fresh, normed_b, keyval_cot, gain_cot)

def reference(saved, cot_in, weights, gains, lengths, segments):
    records = {}
    finals = [[None] * N_FSDP for section in range(N_PIPE)]
    for member in range(N_FSDP):
        for item in range(N_PIPE):
            carried = cot_in[item, member]
            for tick in range(TICKS):
                section = (item - tick) % N_PIPE
                layer = item % 2 * N_PIPE + item - tick
                if layer >= 0:
                    stretch = layer // N_PIPE
                    carried, normed_b, keyval_cot, gain_cot = layer_back(saved[section, member, tick], carried, gains[stretch, section], weights[stretch, section], lengths[item, member], segments[item, member])
                    entry_key = (stretch, section, member)
                    if entry_key in records:
                        records[entry_key].append((normed_b, keyval_cot, gain_cot))
                    else:
                        records[entry_key] = [(normed_b, keyval_cot, gain_cot)]
            finals[(item - TICKS + 1) % N_PIPE][member] = carried
    cot_out = jnp.stack([jnp.stack(row) for row in finals])
    kv_stretches = []
    gain_stretches = []
    for stretch in range(2):
        kv_sections = []
        gain_sections = []
        for section in range(N_PIPE):
            kv_total = jnp.zeros((D, KVW), jnp.float32)
            gain_total = jnp.zeros((D,), jnp.float32)
            for member in range(N_FSDP):
                entry_key = (stretch, section, member)
                entries = records[entry_key] if entry_key in records else []
                if entries:
                    normed_all = jnp.concatenate([entry[0] for entry in entries], axis=0)
                    cot_all = jnp.concatenate([entry[1] for entry in entries], axis=0)
                    kv_part = jnp.dot(normed_all.T, cot_all, preferred_element_type=jnp.float32)
                    gain_part = entries[0][2]
                    for entry in entries[1:]:
                        gain_part = gain_part + entry[2]
                    kv_total = kv_total + lax.optimization_barrier(kv_part.astype(jnp.bfloat16)).astype(jnp.float32)
                    gain_total = gain_total + lax.optimization_barrier(gain_part.astype(jnp.bfloat16)).astype(jnp.float32)
            kv_sections.append(kv_total.astype(jnp.bfloat16))
            gain_sections.append(gain_total.astype(jnp.bfloat16))
        kv_stretches.append(jnp.stack(kv_sections))
        gain_stretches.append(jnp.stack(gain_sections))
    return (cot_out, jnp.stack(kv_stretches), jnp.stack(gain_stretches))
```

```python
import functools

import jax
import jax.numpy as jnp
from jax import lax
from jax.experimental import pallas as pl
from jax.experimental.pallas import tpu as pltpu
from jax.sharding import PartitionSpec as P

HEAD_SIZE = 128
KEY_VALUE_HEADS = 4
TICKS = 3
EPS = 1e-05
MESH = pl.DeviceIdType.MESH
LIMIT = 56 * 1024 * 1024


def passed_along(value, axis, by):
    size = lax.axis_size(axis)
    return lax.ppermute(value, axis, [(i, (i + by) % size) for i in range(size)])


def greet_all(n, me):
    barrier = pltpu.get_barrier_semaphore()

    def greet(k, _):
        pl.semaphore_signal(
            barrier, inc=1, device_id={"fsdp": lax.rem(me + k, n)}, device_id_type=MESH
        )
        return 0

    lax.fori_loop(1, n, greet, 0)
    pl.semaphore_wait(barrier, n - 1)


def to_peer(src, dst, send, recv, peer):
    return pltpu.make_async_remote_copy(
        src_ref=src,
        dst_ref=dst,
        send_sem=send,
        recv_sem=recv,
        device_id={"fsdp": peer},
        device_id_type=MESH,
    )


def stretch_of(section, tick, sections):
    item = lax.rem(section + tick, sections)
    layer = lax.rem(item, 2) * sections + item - tick
    return lax.div(jnp.maximum(layer, 0), sections)


def front_kernel(
    n, sections, saved, w, g, kv, cols, gall, part, ret, xs, xr, gs, gr, ps, pr
):
    me = lax.axis_index("fsdp")
    section = lax.axis_index("pipe")
    width = w.shape[1]
    greet_all(n, me)

    def column_copy(k):
        peer = lax.rem(me + k, n)
        at = pl.ds(pl.multiple_of(peer * width, width), width)
        return to_peer(saved.at[:, :, at], cols.at[k], xs.at[k], xr.at[k], peer)

    def gain_copy(k):
        peer = lax.rem(me + k, n)
        return to_peer(g, gall.at[me], gs.at[k], gr.at[k], peer)

    def back_copy(k):
        peer = lax.rem(me - k + n, n)
        return to_peer(part.at[k], ret.at[k], ps.at[k], pr.at[k], peer)

    def send(k, _):
        column_copy(k).start()
        gain_copy(k).start()
        return 0

    lax.fori_loop(1, n, send, 0)
    gall[me] = g[...]
    cols[0] = saved[:, :, pl.ds(pl.multiple_of(me * width, width), width)]

    def share(k, tick):
        stretch = stretch_of(section, tick, sections)
        gain = g[pl.ds(stretch, 1), :].astype(jnp.float32)
        left = (cols[k, tick].astype(jnp.float32) * gain).astype(jnp.bfloat16)
        return jnp.dot(left, w[stretch], preferred_element_type=jnp.float32)

    for tick in range(TICKS):
        kv[tick] = share(0, tick)

    def answer(k, _):
        column_copy(k).wait_recv()
        for tick in range(TICKS):
            part[k, tick] = share(k, tick).astype(jnp.bfloat16)
        back_copy(k).start()
        return 0

    lax.fori_loop(1, n, answer, 0)

    def collect(k, _):
        back_copy(k).wait_recv()
        kv[...] += ret[k].astype(jnp.float32)
        return 0

    lax.fori_loop(1, n, collect, 0)

    def finish(k, _):
        column_copy(k).wait_send()
        gain_copy(k).wait()
        back_copy(k).wait_send()
        return 0

    lax.fori_loop(1, n, finish, 0)


def front(n, sections, saved, w, g):
    ticks, rows, model = saved.shape
    width, kvw = w.shape[1:]
    vmem = pl.BlockSpec(memory_space=pltpu.VMEM)
    return pl.pallas_call(
        functools.partial(front_kernel, n, sections),
        out_shape=(
            jax.ShapeDtypeStruct((ticks, rows, kvw), jnp.float32),
            jax.ShapeDtypeStruct((n, ticks, rows, width), jnp.bfloat16),
            jax.ShapeDtypeStruct((n, 2, width), jnp.float32),
        ),
        in_specs=[vmem] * 3,
        out_specs=(vmem,) * 3,
        scratch_shapes=[
            pltpu.VMEM((n, ticks, rows, kvw), jnp.bfloat16),
            pltpu.VMEM((n, ticks, rows, kvw), jnp.bfloat16),
        ]
        + [pltpu.SemaphoreType.DMA((n,))] * 6,
        compiler_params=pltpu.CompilerParams(
            collective_id=0, has_side_effects=True, vmem_limit_bytes=LIMIT
        ),
    )(saved, w, g)


def back_kernel(n, sections, tick, kc, w, rows_all, total, part, ks, kr, ps, pr):
    me = lax.axis_index("fsdp")
    section = lax.axis_index("pipe")
    width = w.shape[1]
    stretch = stretch_of(section, tick, sections)
    mine = pl.ds(pl.multiple_of(me * width, width), width)
    greet_all(n, me)

    def row_copy(k):
        return to_peer(kc, rows_all.at[k], ks.at[k], kr.at[k], lax.rem(me + k, n))

    def back_copy(k):
        peer = lax.rem(me - k + n, n)
        return to_peer(part.at[k], total.at[:, mine], ps.at[k], pr.at[k], peer)

    def send(k, _):
        row_copy(k).start()
        return 0

    lax.fori_loop(1, n, send, 0)
    rows_all[0] = kc[...]

    def share(k):
        return lax.dot_general(
            rows_all[k], w[stretch], (((1,), (1,)), ((), ())),
            preferred_element_type=jnp.float32,
        ).astype(jnp.bfloat16)

    total[:, mine] = share(0)

    def answer(k, _):
        row_copy(k).wait_recv()
        part[k] = share(k)
        back_copy(k).start()
        return 0

    lax.fori_loop(1, n, answer, 0)

    def finish(k, _):
        row_copy(k).wait_send()
        back_copy(k).wait()
        return 0

    lax.fori_loop(1, n, finish, 0)


def back(n, sections, tick, kc, w):
    rows, kvw = kc.shape
    width = w.shape[1]
    vmem = pl.BlockSpec(memory_space=pltpu.VMEM)
    return pl.pallas_call(
        functools.partial(back_kernel, n, sections, tick),
        out_shape=(
            jax.ShapeDtypeStruct((n, rows, kvw), jnp.bfloat16),
            jax.ShapeDtypeStruct((rows, n * width), jnp.bfloat16),
        ),
        in_specs=[vmem] * 2,
        out_specs=(vmem,) * 2,
        scratch_shapes=[pltpu.VMEM((n, rows, width), jnp.bfloat16)]
        + [pltpu.SemaphoreType.DMA((n,))] * 4,
        compiler_params=pltpu.CompilerParams(
            collective_id=1 + tick, has_side_effects=True, vmem_limit_bytes=LIMIT
        ),
    )(kc, w)


def gain_kernel(n, sums, out, got, ss, sr):
    me = lax.axis_index("fsdp")
    greet_all(n, me)

    def copy(k):
        peer = lax.rem(me + k, n)
        return to_peer(sums.at[peer], got.at[k], ss.at[k], sr.at[k], peer)

    def send(k, _):
        copy(k).start()
        return 0

    lax.fori_loop(1, n, send, 0)
    out[...] = sums[me]

    def collect(k, _):
        copy(k).wait()
        out[...] += got[k]
        return 0

    lax.fori_loop(1, n, collect, 0)


def gain_sums(n, sums):
    vmem = pl.BlockSpec(memory_space=pltpu.VMEM)
    return pl.pallas_call(
        functools.partial(gain_kernel, n),
        out_shape=jax.ShapeDtypeStruct(sums.shape[1:], jnp.float32),
        in_specs=[vmem],
        out_specs=vmem,
        scratch_shapes=[pltpu.VMEM(sums.shape, jnp.float32)]
        + [pltpu.SemaphoreType.DMA((n,))] * 2,
        compiler_params=pltpu.CompilerParams(
            collective_id=1 + TICKS, has_side_effects=True, vmem_limit_bytes=LIMIT
        ),
    )(sums)


def normalize(resid, gain):
    factor = lax.rsqrt(jnp.mean(resid * resid, axis=-1, keepdims=True) + EPS)
    return resid * factor * gain


def attend(resid, normalized_input, key_value_pair, length, segment):
    item_count = resid.shape[0]
    model_width = resid.shape[1]
    query_groups = model_width // HEAD_SIZE // KEY_VALUE_HEADS
    query_rows = normalized_input.astype(jnp.bfloat16).reshape(
        item_count, KEY_VALUE_HEADS, query_groups, HEAD_SIZE
    )
    key_rows = (
        key_value_pair[:, : KEY_VALUE_HEADS * HEAD_SIZE]
        .astype(jnp.bfloat16)
        .reshape(item_count, KEY_VALUE_HEADS, HEAD_SIZE)
    )
    value_rows = (
        key_value_pair[:, KEY_VALUE_HEADS * HEAD_SIZE :]
        .astype(jnp.bfloat16)
        .reshape(item_count, KEY_VALUE_HEADS, HEAD_SIZE)
    )
    scores = jnp.einsum(
        "pkgd,qkd->kgpq", query_rows, key_rows, preferred_element_type=jnp.float32
    ) * HEAD_SIZE ** (-0.5)
    place = jnp.arange(item_count, dtype=jnp.int32)
    allowed = (
        (segment[:, None] == segment[None, :])
        & (place[None, :] <= place[:, None])
        & (place[None, :] < length)
    )
    allowed = allowed | (place[:, None] == place[None, :])
    scores = jnp.where(allowed, scores, -1e30)
    peak = jnp.max(scores, axis=-1, keepdims=True)
    expo = jnp.exp(scores - peak)
    probs = (expo / jnp.sum(expo, axis=-1, keepdims=True)).astype(jnp.bfloat16)
    mixed = jnp.einsum(
        "kgpq,qkd->pkgd", probs, value_rows, preferred_element_type=jnp.float32
    ).reshape(item_count, model_width)
    valid = (place < length).astype(jnp.float32)
    return resid + mixed * valid[:, None]


def body(saved, cot_in, weights, gains, lengths, segments):
    sections = lax.axis_size("pipe")
    n = lax.axis_size("fsdp")
    section = lax.axis_index("pipe")
    carried = cot_in[0, 0]
    model = carried.shape[-1]
    w, g = weights[:, 0], gains[:, 0]
    own_gain = g.astype(jnp.float32)
    kv, cols, gall = front(n, sections, saved[0, 0], w, own_gain)
    whole_g = jnp.swapaxes(gall, 0, 1).reshape(2, model)
    acc_gain = jnp.zeros((2, model), jnp.float32)
    right = []
    for tick in range(TICKS):
        item = (section + tick) % sections
        layer = item % 2 * sections + item - tick
        active = layer >= 0
        stretch = jnp.maximum(layer, 0) // sections
        length = lengths[item, 0]
        segment = segments[item, 0]
        resid = saved[0, 0, tick].astype(jnp.float32)
        factor = lax.rsqrt(jnp.mean(resid * resid, axis=-1, keepdims=True) + EPS)
        normalized_input, front_pull = jax.vjp(normalize, resid, whole_g[stretch])

        def inner(first, second, third):
            return attend(first, second, third, length, segment)

        _, pull = jax.vjp(inner, resid, normalized_input, kv[tick] * factor)
        direct, normed_cot, keyval_cot = pull(carried.astype(jnp.float32))
        scaled = jnp.where(active, keyval_cot * factor, 0.0).astype(jnp.bfloat16)
        rows_all, product = back(n, sections, tick, scaled, w)
        right.append((rows_all, active & (stretch == 0), active & (stretch == 1)))
        normed_total = normed_cot + product.astype(jnp.float32) / factor
        resid_cot, gain_cot = front_pull(normed_total)
        acc_gain = acc_gain.at[stretch].add(jnp.where(active, gain_cot, 0.0))
        carried = jnp.where(active, (direct + resid_cot).astype(jnp.bfloat16), carried)
        if tick + 1 < TICKS:
            carried = passed_along(carried, "pipe", -1)
    width = w.shape[1]
    sums = jnp.swapaxes(acc_gain.reshape(2, n, width), 0, 1)
    grad_gain = gain_sums(n, sums).astype(jnp.bfloat16)[:, None]
    left = cols.reshape(-1, width)
    grads = []
    for which in (1, 2):
        block = jnp.stack(
            [jnp.where(r[which], r[0], jnp.zeros_like(r[0])) for r in right], axis=1
        ).reshape(left.shape[0], -1)
        grads.append(
            lax.dot_general(
                left, block, (((0,), (0,)), ((), ())), preferred_element_type=jnp.float32
            )
        )
    grad_kv = (jnp.stack(grads) * own_gain[:, :, None]).astype(jnp.bfloat16)[:, None]
    return (carried[None, None], grad_kv, grad_gain)


def solution(mesh):
    in_specs = (
        P("pipe", "fsdp", None, None, None),
        P("pipe", "fsdp", None, None),
        P(None, "pipe", "fsdp", None),
        P(None, "pipe", "fsdp"),
        P(None, "fsdp"),
        P(None, "fsdp", None),
    )
    out_specs = (
        P("pipe", "fsdp", None, None),
        P(None, "pipe", "fsdp", None),
        P(None, "pipe", "fsdp"),
    )
    return jax.shard_map(body, mesh=mesh, in_specs=in_specs, out_specs=out_specs, check_vma=False)
```

```python
import functools

import jax
import jax.numpy as jnp
from jax import lax
from jax.experimental import pallas as pl
from jax.experimental.pallas import tpu as pltpu
from jax.sharding import PartitionSpec as P

HEAD_SIZE = 128
KEY_VALUE_HEADS = 4
TICKS = 3
EPS = 1e-05
MESH = pl.DeviceIdType.MESH
LIMIT = 56 * 1024 * 1024


def passed_along(value, axis, by):
    size = lax.axis_size(axis)
    return lax.ppermute(value, axis, [(i, (i + by) % size) for i in range(size)])


def greet_all(n, me):
    barrier = pltpu.get_barrier_semaphore()

    def greet(k, _):
        pl.semaphore_signal(
            barrier, inc=1, device_id={"fsdp": lax.rem(me + k, n)}, device_id_type=MESH
        )
        return 0

    lax.fori_loop(1, n, greet, 0)
    pl.semaphore_wait(barrier, n - 1)


def to_peer(src, dst, send, recv, peer):
    return pltpu.make_async_remote_copy(
        src_ref=src,
        dst_ref=dst,
        send_sem=send,
        recv_sem=recv,
        device_id={"fsdp": peer},
        device_id_type=MESH,
    )


def stretch_of(section, tick, sections):
    item = lax.rem(section + tick, sections)
    layer = lax.rem(item, 2) * sections + item - tick
    return lax.div(jnp.maximum(layer, 0), sections)


def front_kernel(
    n, sections, saved, w, g, kv, cols, gall, w2,
    pair_g, wide, part, ret, xs, xr, fs, fr, ps, pr, gs, gr, ws, wr, qs, qr
):
    me = lax.axis_index("fsdp")
    section = lax.axis_index("pipe")
    width = w.shape[1]
    steps = n // 2
    place, half = lax.div(me, 2), lax.rem(me, 2)
    buddy = place * 2 + 1 - half
    first = stretch_of(section, 0, sections)
    second = 1 - first
    late = stretch_of(section, 2, sections)
    own_rows = pl.ds(pl.multiple_of(half * width, width), width)
    buddy_rows = pl.ds(pl.multiple_of((1 - half) * width, width), width)
    greet_all(n, me)

    def weight_copy(i, stretch):
        return to_peer(w.at[stretch], w2.at[stretch, own_rows], ws.at[i], wr.at[i], buddy)

    def pair_gain_copy():
        return to_peer(g, pair_g.at[half], qs, qr, buddy)

    def column_copy(k, tick):
        to = lax.rem(place + k, steps)
        at = pl.ds(pl.multiple_of(to * 2 * width, 2 * width), 2 * width)
        return to_peer(
            saved.at[tick, :, at], wide.at[k, tick], xs.at[k, tick], xr.at[k, tick],
            to * 2 + half,
        )

    def half_copy(k, tick):
        return to_peer(
            wide.at[k, tick, :, buddy_rows], cols.at[1, k, tick],
            fs.at[k, tick], fr.at[k, tick], buddy,
        )

    def gain_copy(k):
        peer = lax.rem(me + k, n)
        return to_peer(g, gall.at[me], gs.at[k], gr.at[k], peer)

    def back_copy(k, tick):
        to = lax.rem(place - k + steps, steps)
        return to_peer(
            part.at[k, tick], ret.at[k, tick], ps.at[k, tick], pr.at[k, tick],
            to * 2 + half,
        )

    pair_gain_copy().start()
    weight_copy(0, first).start()
    for tick in (0, 2, 1):

        def send(k, _, tick=tick):
            column_copy(k, tick).start()
            return 0

        lax.fori_loop(1, steps, send, 0)
    weight_copy(1, second).start()

    def send_gain(k, _):
        gain_copy(k).start()
        return 0

    lax.fori_loop(1, n, send_gain, 0)
    gall[me] = g[...]
    pair_g[half] = g[...]
    at = pl.ds(pl.multiple_of(place * 2 * width, 2 * width), 2 * width)
    wide[0] = saved[:, :, at]
    w2[:, own_rows, :] = w[...]
    for tick in (0, 2, 1):
        half_copy(0, tick).start()
    pair_gain_copy().wait_recv()

    def share(k, tick):
        stretch = stretch_of(section, tick, sections)
        total = None
        for side in range(2):
            at = pl.ds(side * width, width)
            gain = pair_g[side, pl.ds(stretch, 1), :]
            left = (wide[k, tick, :, at].astype(jnp.float32) * gain).astype(jnp.bfloat16)
            term = jnp.dot(left, w2[stretch, at, :], preferred_element_type=jnp.float32)
            total = term if total is None else total + term
        return total

    weight_copy(0, first).wait_recv()
    for tick in (0, 2, 1):
        if tick == 2:

            @pl.when(late != first)
            def _():
                weight_copy(1, second).wait_recv()

        if tick == 1:

            @pl.when(late == first)
            def _():
                weight_copy(1, second).wait_recv()

        def answer(k, _, tick=tick):
            column_copy(k, tick).wait_recv()
            half_copy(k, tick).start()
            part[k, tick] = share(k, tick).astype(jnp.bfloat16)
            back_copy(k, tick).start()
            return 0

        lax.fori_loop(1, steps, answer, 0)
        kv[tick] = share(0, tick)

    def own_half(k, _):
        cols[0, k] = wide[k, :, :, own_rows]
        return 0

    lax.fori_loop(0, steps, own_half, 0)
    for tick in (0, 2, 1):

        def collect(k, _, tick=tick):
            back_copy(k, tick).wait_recv()
            kv[tick] += ret[k, tick].astype(jnp.float32)
            return 0

        lax.fori_loop(1, steps, collect, 0)
        half_copy(0, tick).wait()

        def finish(k, _, tick=tick):
            column_copy(k, tick).wait_send()
            half_copy(k, tick).wait()
            back_copy(k, tick).wait_send()
            return 0

        lax.fori_loop(1, steps, finish, 0)

    def finish_gain(k, _):
        gain_copy(k).wait()
        return 0

    lax.fori_loop(1, n, finish_gain, 0)
    pair_gain_copy().wait_send()
    weight_copy(0, first).wait_send()
    weight_copy(1, second).wait_send()


def front(n, sections, saved, w, g):
    ticks, rows, model = saved.shape
    width, kvw = w.shape[1:]
    steps = n // 2
    vmem = pl.BlockSpec(memory_space=pltpu.VMEM)
    dma = pltpu.SemaphoreType.DMA
    return pl.pallas_call(
        functools.partial(front_kernel, n, sections),
        out_shape=(
            jax.ShapeDtypeStruct((ticks, rows, kvw), jnp.float32),
            jax.ShapeDtypeStruct((2, steps, ticks, rows, width), jnp.bfloat16),
            jax.ShapeDtypeStruct((n, 2, width), jnp.float32),
            jax.ShapeDtypeStruct((2, 2 * width, kvw), jnp.bfloat16),
        ),
        in_specs=[vmem] * 3,
        out_specs=(vmem,) * 4,
        scratch_shapes=[
            pltpu.VMEM((2, 2, width), jnp.float32),
            pltpu.VMEM((steps, ticks, rows, 2 * width), jnp.bfloat16),
            pltpu.VMEM((steps, ticks, rows, kvw), jnp.bfloat16),
            pltpu.VMEM((steps, ticks, rows, kvw), jnp.bfloat16),
        ]
        + [dma((steps, ticks))] * 6
        + [dma((n,))] * 2
        + [dma((2,))] * 2
        + [dma] * 2,
        compiler_params=pltpu.CompilerParams(
            collective_id=0, has_side_effects=True, vmem_limit_bytes=LIMIT
        ),
    )(saved, w, g)


def back_kernel(
    n, sections, tick, kc, w2, rows_all, total, part, ks, kr, fs, fr, ps, pr
):
    me = lax.axis_index("fsdp")
    section = lax.axis_index("pipe")
    wide = w2.shape[1]
    steps = n // 2
    place, half = lax.div(me, 2), lax.rem(me, 2)
    buddy = place * 2 + 1 - half
    stretch = stretch_of(section, tick, sections)
    mine = pl.ds(pl.multiple_of(place * wide, wide), wide)
    greet_all(n, me)

    def row_copy(k):
        to = lax.rem(place + k, steps) * 2 + half
        return to_peer(kc, rows_all.at[0, k], ks.at[k], kr.at[k], to)

    def own_copy():
        return to_peer(kc, rows_all.at[1, 0], fs.at[0], fr.at[0], buddy)

    def pair_copy(k):
        return to_peer(rows_all.at[0, k], rows_all.at[1, k], fs.at[k], fr.at[k], buddy)

    def back_copy(k):
        to = lax.rem(place - k + steps, steps) * 2 + half
        return to_peer(part.at[k], total.at[:, mine], ps.at[k], pr.at[k], to)

    def send(k, _):
        row_copy(k).start()
        return 0

    lax.fori_loop(1, steps, send, 0)
    own_copy().start()
    rows_all[0, 0] = kc[...]

    def share(k):
        return lax.dot_general(
            rows_all[0, k], w2[stretch], (((1,), (1,)), ((), ())),
            preferred_element_type=jnp.float32,
        ).astype(jnp.bfloat16)

    total[:, mine] = share(0)

    def answer(k, _):
        row_copy(k).wait_recv()
        pair_copy(k).start()
        part[k] = share(k)
        back_copy(k).start()
        return 0

    lax.fori_loop(1, steps, answer, 0)
    own_copy().wait()

    def finish(k, _):
        row_copy(k).wait_send()
        pair_copy(k).wait()
        back_copy(k).wait()
        return 0

    lax.fori_loop(1, steps, finish, 0)


def back(n, sections, tick, kc, w2):
    rows, kvw = kc.shape
    wide = w2.shape[1]
    steps = n // 2
    vmem = pl.BlockSpec(memory_space=pltpu.VMEM)
    return pl.pallas_call(
        functools.partial(back_kernel, n, sections, tick),
        out_shape=(
            jax.ShapeDtypeStruct((2, steps, rows, kvw), jnp.bfloat16),
            jax.ShapeDtypeStruct((rows, steps * wide), jnp.bfloat16),
        ),
        in_specs=[vmem] * 2,
        out_specs=(vmem,) * 2,
        scratch_shapes=[pltpu.VMEM((steps, rows, wide), jnp.bfloat16)]
        + [pltpu.SemaphoreType.DMA((steps,))] * 6,
        compiler_params=pltpu.CompilerParams(
            collective_id=1 + tick, has_side_effects=True, vmem_limit_bytes=LIMIT
        ),
    )(kc, w2)


def gain_kernel(n, sums, out, got, ss, sr):
    me = lax.axis_index("fsdp")
    greet_all(n, me)

    def copy(k):
        peer = lax.rem(me + k, n)
        return to_peer(sums.at[peer], got.at[k], ss.at[k], sr.at[k], peer)

    def send(k, _):
        copy(k).start()
        return 0

    lax.fori_loop(1, n, send, 0)
    out[...] = sums[me]

    def collect(k, _):
        copy(k).wait()
        out[...] += got[k]
        return 0

    lax.fori_loop(1, n, collect, 0)


def gain_sums(n, sums):
    vmem = pl.BlockSpec(memory_space=pltpu.VMEM)
    return pl.pallas_call(
        functools.partial(gain_kernel, n),
        out_shape=jax.ShapeDtypeStruct(sums.shape[1:], jnp.float32),
        in_specs=[vmem],
        out_specs=vmem,
        scratch_shapes=[pltpu.VMEM(sums.shape, jnp.float32)]
        + [pltpu.SemaphoreType.DMA((n,))] * 2,
        compiler_params=pltpu.CompilerParams(
            collective_id=1 + TICKS, has_side_effects=True, vmem_limit_bytes=LIMIT
        ),
    )(sums)


def normalize(resid, gain):
    factor = lax.rsqrt(jnp.mean(resid * resid, axis=-1, keepdims=True) + EPS)
    return resid * factor * gain


def attend(resid, normalized_input, key_value_pair, length, segment):
    item_count = resid.shape[0]
    model_width = resid.shape[1]
    query_groups = model_width // HEAD_SIZE // KEY_VALUE_HEADS
    query_rows = normalized_input.astype(jnp.bfloat16).reshape(
        item_count, KEY_VALUE_HEADS, query_groups, HEAD_SIZE
    )
    key_rows = (
        key_value_pair[:, : KEY_VALUE_HEADS * HEAD_SIZE]
        .astype(jnp.bfloat16)
        .reshape(item_count, KEY_VALUE_HEADS, HEAD_SIZE)
    )
    value_rows = (
        key_value_pair[:, KEY_VALUE_HEADS * HEAD_SIZE :]
        .astype(jnp.bfloat16)
        .reshape(item_count, KEY_VALUE_HEADS, HEAD_SIZE)
    )
    scores = jnp.einsum(
        "pkgd,qkd->kgpq", query_rows, key_rows, preferred_element_type=jnp.float32
    ) * HEAD_SIZE ** (-0.5)
    place = jnp.arange(item_count, dtype=jnp.int32)
    allowed = (
        (segment[:, None] == segment[None, :])
        & (place[None, :] <= place[:, None])
        & (place[None, :] < length)
    )
    allowed = allowed | (place[:, None] == place[None, :])
    scores = jnp.where(allowed, scores, -1e30)
    peak = jnp.max(scores, axis=-1, keepdims=True)
    expo = jnp.exp(scores - peak)
    probs = (expo / jnp.sum(expo, axis=-1, keepdims=True)).astype(jnp.bfloat16)
    mixed = jnp.einsum(
        "kgpq,qkd->pkgd", probs, value_rows, preferred_element_type=jnp.float32
    ).reshape(item_count, model_width)
    valid = (place < length).astype(jnp.float32)
    return resid + mixed * valid[:, None]


def body(saved, cot_in, weights, gains, lengths, segments):
    sections = lax.axis_size("pipe")
    n = lax.axis_size("fsdp")
    section = lax.axis_index("pipe")
    carried = cot_in[0, 0]
    model = carried.shape[-1]
    w, g = weights[:, 0], gains[:, 0]
    own_gain = g.astype(jnp.float32)
    kv, cols, gall, w2 = front(n, sections, saved[0, 0], w, own_gain)
    whole_g = jnp.swapaxes(gall, 0, 1).reshape(2, model)
    acc_gain = jnp.zeros((2, model), jnp.float32)
    right = []
    for tick in range(TICKS):
        item = (section + tick) % sections
        layer = item % 2 * sections + item - tick
        active = layer >= 0
        stretch = jnp.maximum(layer, 0) // sections
        length = lengths[item, 0]
        segment = segments[item, 0]
        resid = saved[0, 0, tick].astype(jnp.float32)
        factor = lax.rsqrt(jnp.mean(resid * resid, axis=-1, keepdims=True) + EPS)
        normalized_input, front_pull = jax.vjp(normalize, resid, whole_g[stretch])

        def inner(first, second, third):
            return attend(first, second, third, length, segment)

        _, pull = jax.vjp(inner, resid, normalized_input, kv[tick] * factor)
        direct, normed_cot, keyval_cot = pull(carried.astype(jnp.float32))
        scaled = jnp.where(active, keyval_cot * factor, 0.0).astype(jnp.bfloat16)
        rows_all, product = back(n, sections, tick, scaled, w2)
        right.append((rows_all, active & (stretch == 0), active & (stretch == 1)))
        normed_total = normed_cot + product.astype(jnp.float32) / factor
        resid_cot, gain_cot = front_pull(normed_total)
        acc_gain = acc_gain.at[stretch].add(jnp.where(active, gain_cot, 0.0))
        carried = jnp.where(active, (direct + resid_cot).astype(jnp.bfloat16), carried)
        if tick + 1 < TICKS:
            carried = passed_along(carried, "pipe", -1)
    width = w.shape[1]
    sums = jnp.swapaxes(acc_gain.reshape(2, n, width), 0, 1)
    grad_gain = gain_sums(n, sums).astype(jnp.bfloat16)[:, None]
    left = cols.reshape(-1, width)
    grads = []
    for which in (1, 2):
        block = jnp.stack(
            [jnp.where(r[which], r[0], jnp.zeros_like(r[0])) for r in right], axis=2
        ).reshape(left.shape[0], -1)
        grads.append(
            lax.dot_general(
                left, block, (((0,), (0,)), ((), ())), preferred_element_type=jnp.float32
            )
        )
    grad_kv = (jnp.stack(grads) * own_gain[:, :, None]).astype(jnp.bfloat16)[:, None]
    return (carried[None, None], grad_kv, grad_gain)


def solution(mesh):
    in_specs = (
        P("pipe", "fsdp", None, None, None),
        P("pipe", "fsdp", None, None),
        P(None, "pipe", "fsdp", None),
        P(None, "pipe", "fsdp"),
        P(None, "fsdp"),
        P(None, "fsdp", None),
    )
    out_specs = (
        P("pipe", "fsdp", None, None),
        P(None, "pipe", "fsdp", None),
        P(None, "pipe", "fsdp"),
    )
    return jax.shard_map(body, mesh=mesh, in_specs=in_specs, out_specs=out_specs, check_vma=False)
```

```python
import functools

import jax
import jax.numpy as jnp
from jax import lax
from jax.experimental import pallas as pl
from jax.experimental.pallas import tpu as pltpu
from jax.sharding import PartitionSpec as P

HEAD_SIZE = 128
KEY_VALUE_HEADS = 4
TICKS = 3
EPS = 1e-05
MESH = pl.DeviceIdType.MESH
LIMIT = 56 * 1024 * 1024


def passed_along(value, axis, by):
    size = lax.axis_size(axis)
    return lax.ppermute(value, axis, [(i, (i + by) % size) for i in range(size)])


def greet_all(n, me):
    barrier = pltpu.get_barrier_semaphore()

    def greet(k, _):
        pl.semaphore_signal(
            barrier, inc=1, device_id={"fsdp": lax.rem(me + k, n)}, device_id_type=MESH
        )
        return 0

    lax.fori_loop(1, n, greet, 0)
    pl.semaphore_wait(barrier, n - 1)


def to_peer(src, dst, send, recv, peer):
    return pltpu.make_async_remote_copy(
        src_ref=src,
        dst_ref=dst,
        send_sem=send,
        recv_sem=recv,
        device_id={"fsdp": peer},
        device_id_type=MESH,
    )


def stretch_of(section, tick, sections):
    item = lax.rem(section + tick, sections)
    layer = lax.rem(item, 2) * sections + item - tick
    return lax.div(jnp.maximum(layer, 0), sections)


def front_kernel(
    n, sections, saved, w, g, kv, cols, gall, w2,
    pair_g, wide, part, ret, xs, xr, fs, fr, ps, pr, gs, gr, ws, wr, qs, qr
):
    me = lax.axis_index("fsdp")
    section = lax.axis_index("pipe")
    width = w.shape[1]
    steps = n // 2
    place, half = lax.div(me, 2), lax.rem(me, 2)
    buddy = place * 2 + 1 - half
    first = stretch_of(section, 0, sections)
    second = 1 - first
    late = stretch_of(section, 2, sections)
    own_rows = pl.ds(pl.multiple_of(half * width, width), width)
    buddy_rows = pl.ds(pl.multiple_of((1 - half) * width, width), width)
    greet_all(n, me)

    def weight_copy(i, stretch):
        return to_peer(w.at[stretch], w2.at[stretch, own_rows], ws.at[i], wr.at[i], buddy)

    def pair_gain_copy():
        return to_peer(g, pair_g.at[half], qs, qr, buddy)

    def column_copy(k, tick):
        to = lax.rem(place + k, steps)
        at = pl.ds(pl.multiple_of(to * 2 * width, 2 * width), 2 * width)
        return to_peer(
            saved.at[tick, :, at], wide.at[k, tick], xs.at[k, tick], xr.at[k, tick],
            to * 2 + half,
        )

    def half_copy(k, tick):
        return to_peer(
            wide.at[k, tick, :, buddy_rows], cols.at[1, k, tick],
            fs.at[k, tick], fr.at[k, tick], buddy,
        )

    def gain_copy(k):
        peer = lax.rem(me + k, n)
        return to_peer(g, gall.at[me], gs.at[k], gr.at[k], peer)

    def back_copy(k, tick):
        to = lax.rem(place - k + steps, steps)
        return to_peer(
            part.at[k, tick], ret.at[k, tick], ps.at[k, tick], pr.at[k, tick],
            to * 2 + half,
        )

    pair_gain_copy().start()
    weight_copy(0, first).start()
    for tick in (0, 2, 1):

        def send(k, _, tick=tick):
            column_copy(k, tick).start()
            return 0

        lax.fori_loop(1, steps, send, 0)
    weight_copy(1, second).start()

    def send_gain(k, _):
        gain_copy(k).start()
        return 0

    lax.fori_loop(1, n, send_gain, 0)
    gall[me] = g[...]
    pair_g[half] = g[...]
    at = pl.ds(pl.multiple_of(place * 2 * width, 2 * width), 2 * width)
    wide[0] = saved[:, :, at]
    w2[:, own_rows, :] = w[...]
    for tick in (0, 2, 1):
        half_copy(0, tick).start()
    pair_gain_copy().wait_recv()

    def share(k, tick):
        stretch = stretch_of(section, tick, sections)
        total = None
        for side in range(2):
            at = pl.ds(side * width, width)
            gain = pair_g[side, pl.ds(stretch, 1), :]
            left = (wide[k, tick, :, at].astype(jnp.float32) * gain).astype(jnp.bfloat16)
            term = jnp.dot(left, w2[stretch, at, :], preferred_element_type=jnp.float32)
            total = term if total is None else total + term
        return total

    weight_copy(0, first).wait_recv()
    for tick in (0, 2, 1):
        if tick == 2:

            @pl.when(late != first)
            def _():
                weight_copy(1, second).wait_recv()

        if tick == 1:

            @pl.when(late == first)
            def _():
                weight_copy(1, second).wait_recv()

        def answer(k, _, tick=tick):
            column_copy(k, tick).wait_recv()
            half_copy(k, tick).start()
            part[k, tick] = share(k, tick).astype(jnp.bfloat16)
            back_copy(k, tick).start()
            return 0

        lax.fori_loop(1, steps, answer, 0)
        kv[tick] = share(0, tick)

    def own_half(k, _):
        cols[0, k] = wide[k, :, :, own_rows]
        return 0

    lax.fori_loop(0, steps, own_half, 0)
    for tick in (0, 2, 1):

        def collect(k, _, tick=tick):
            back_copy(k, tick).wait_recv()
            kv[tick] += ret[k, tick].astype(jnp.float32)
            return 0

        lax.fori_loop(1, steps, collect, 0)
        half_copy(0, tick).wait()

        def finish(k, _, tick=tick):
            column_copy(k, tick).wait_send()
            half_copy(k, tick).wait()
            back_copy(k, tick).wait_send()
            return 0

        lax.fori_loop(1, steps, finish, 0)

    def finish_gain(k, _):
        gain_copy(k).wait()
        return 0

    lax.fori_loop(1, n, finish_gain, 0)
    pair_gain_copy().wait_send()
    weight_copy(0, first).wait_send()
    weight_copy(1, second).wait_send()


def front(n, sections, saved, w, g):
    ticks, rows, model = saved.shape
    width, kvw = w.shape[1:]
    steps = n // 2
    vmem = pl.BlockSpec(memory_space=pltpu.VMEM)
    dma = pltpu.SemaphoreType.DMA
    return pl.pallas_call(
        functools.partial(front_kernel, n, sections),
        out_shape=(
            jax.ShapeDtypeStruct((ticks, rows, kvw), jnp.float32),
            jax.ShapeDtypeStruct((2, steps, ticks, rows, width), jnp.bfloat16),
            jax.ShapeDtypeStruct((n, 2, width), jnp.float32),
            jax.ShapeDtypeStruct((2, 2 * width, kvw), jnp.bfloat16),
        ),
        in_specs=[vmem] * 3,
        out_specs=(vmem,) * 4,
        scratch_shapes=[
            pltpu.VMEM((2, 2, width), jnp.float32),
            pltpu.VMEM((steps, ticks, rows, 2 * width), jnp.bfloat16),
            pltpu.VMEM((steps, ticks, rows, kvw), jnp.bfloat16),
            pltpu.VMEM((steps, ticks, rows, kvw), jnp.bfloat16),
        ]
        + [dma((steps, ticks))] * 6
        + [dma((n,))] * 2
        + [dma((2,))] * 2
        + [dma] * 2,
        compiler_params=pltpu.CompilerParams(
            collective_id=0, has_side_effects=True, vmem_limit_bytes=LIMIT
        ),
    )(saved, w, g)


def back_kernel(
    n, sections, tick, kc, w2, rows_all, total, part, ks, kr, fs, fr, ps, pr
):
    me = lax.axis_index("fsdp")
    section = lax.axis_index("pipe")
    wide = w2.shape[1]
    steps = n // 2
    place, half = lax.div(me, 2), lax.rem(me, 2)
    buddy = place * 2 + 1 - half
    stretch = stretch_of(section, tick, sections)
    mine = pl.ds(pl.multiple_of(place * wide, wide), wide)
    greet_all(n, me)

    def row_copy(k):
        to = lax.rem(place + k, steps) * 2 + half
        return to_peer(kc, rows_all.at[0, k], ks.at[k], kr.at[k], to)

    def own_copy():
        return to_peer(kc, rows_all.at[1, 0], fs.at[0], fr.at[0], buddy)

    def pair_copy(k):
        return to_peer(rows_all.at[0, k], rows_all.at[1, k], fs.at[k], fr.at[k], buddy)

    def back_copy(k):
        to = lax.rem(place - k + steps, steps) * 2 + half
        return to_peer(part.at[k], total.at[:, mine], ps.at[k], pr.at[k], to)

    def send(k, _):
        row_copy(k).start()
        return 0

    lax.fori_loop(1, steps, send, 0)
    own_copy().start()
    rows_all[0, 0] = kc[...]

    def share(k):
        return lax.dot_general(
            rows_all[0, k], w2[stretch], (((1,), (1,)), ((), ())),
            preferred_element_type=jnp.float32,
        ).astype(jnp.bfloat16)

    total[:, mine] = share(0)

    def answer(k, _):
        row_copy(k).wait_recv()
        pair_copy(k).start()
        part[k] = share(k)
        back_copy(k).start()
        return 0

    lax.fori_loop(1, steps, answer, 0)
    own_copy().wait()

    def finish(k, _):
        row_copy(k).wait_send()
        pair_copy(k).wait()
        back_copy(k).wait()
        return 0

    lax.fori_loop(1, steps, finish, 0)


def back(n, sections, tick, kc, w2):
    rows, kvw = kc.shape
    wide = w2.shape[1]
    steps = n // 2
    vmem = pl.BlockSpec(memory_space=pltpu.VMEM)
    return pl.pallas_call(
        functools.partial(back_kernel, n, sections, tick),
        out_shape=(
            jax.ShapeDtypeStruct((2, steps, rows, kvw), jnp.bfloat16),
            jax.ShapeDtypeStruct((rows, steps * wide), jnp.bfloat16),
        ),
        in_specs=[vmem] * 2,
        out_specs=(vmem,) * 2,
        scratch_shapes=[pltpu.VMEM((steps, rows, wide), jnp.bfloat16)]
        + [pltpu.SemaphoreType.DMA((steps,))] * 6,
        compiler_params=pltpu.CompilerParams(
            collective_id=1 + tick, has_side_effects=True, vmem_limit_bytes=LIMIT
        ),
    )(kc, w2)


def tail_kernel(
    n, sections, sums, cols, first, second, third, g, grad, gain, got, acc, ss, sr
):
    me = lax.axis_index("fsdp")
    section = lax.axis_index("pipe")
    greet_all(n, me)

    def copy(k):
        peer = lax.rem(me + k, n)
        return to_peer(sums.at[peer], got.at[k], ss.at[k], sr.at[k], peer)

    def send(k, _):
        copy(k).start()
        return 0

    lax.fori_loop(1, n, send, 0)
    acc[...] = jnp.zeros_like(acc)
    for tick, rows in enumerate((first, second, third)):
        stretch = stretch_of(section, tick, sections)
        left = cols[:, :, tick].reshape(-1, cols.shape[-1])
        right = rows[...].reshape(left.shape[0], -1)
        acc[stretch] += lax.dot_general(
            left, right, (((0,), (0,)), ((), ())), preferred_element_type=jnp.float32
        )
    grad[...] = (acc[...] * g[...]).astype(jnp.bfloat16)
    gain[...] = sums[me]

    def collect(k, _):
        copy(k).wait()
        gain[...] += got[k]
        return 0

    lax.fori_loop(1, n, collect, 0)


def tail(n, sections, sums, cols, rows, g):
    kvw = rows[0].shape[-1]
    vmem = pl.BlockSpec(memory_space=pltpu.VMEM)
    return pl.pallas_call(
        functools.partial(tail_kernel, n, sections),
        out_shape=(
            jax.ShapeDtypeStruct((2, cols.shape[-1], kvw), jnp.bfloat16),
            jax.ShapeDtypeStruct(sums.shape[1:], jnp.float32),
        ),
        in_specs=[vmem] * 6,
        out_specs=(vmem,) * 2,
        scratch_shapes=[
            pltpu.VMEM(sums.shape, jnp.float32),
            pltpu.VMEM((2, cols.shape[-1], kvw), jnp.float32),
        ]
        + [pltpu.SemaphoreType.DMA((n,))] * 2,
        compiler_params=pltpu.CompilerParams(
            collective_id=1 + TICKS, has_side_effects=True, vmem_limit_bytes=LIMIT
        ),
    )(sums, cols, *rows, g)


def normalize(resid, gain):
    factor = lax.rsqrt(jnp.mean(resid * resid, axis=-1, keepdims=True) + EPS)
    return resid * factor * gain


def attend(resid, normalized_input, key_value_pair, length, segment):
    item_count = resid.shape[0]
    model_width = resid.shape[1]
    query_groups = model_width // HEAD_SIZE // KEY_VALUE_HEADS
    query_rows = normalized_input.astype(jnp.bfloat16).reshape(
        item_count, KEY_VALUE_HEADS, query_groups, HEAD_SIZE
    )
    key_rows = (
        key_value_pair[:, : KEY_VALUE_HEADS * HEAD_SIZE]
        .astype(jnp.bfloat16)
        .reshape(item_count, KEY_VALUE_HEADS, HEAD_SIZE)
    )
    value_rows = (
        key_value_pair[:, KEY_VALUE_HEADS * HEAD_SIZE :]
        .astype(jnp.bfloat16)
        .reshape(item_count, KEY_VALUE_HEADS, HEAD_SIZE)
    )
    scores = jnp.einsum(
        "pkgd,qkd->kgpq", query_rows, key_rows, preferred_element_type=jnp.float32
    ) * HEAD_SIZE ** (-0.5)
    place = jnp.arange(item_count, dtype=jnp.int32)
    allowed = (
        (segment[:, None] == segment[None, :])
        & (place[None, :] <= place[:, None])
        & (place[None, :] < length)
    )
    allowed = allowed | (place[:, None] == place[None, :])
    scores = jnp.where(allowed, scores, -1e30)
    peak = jnp.max(scores, axis=-1, keepdims=True)
    expo = jnp.exp(scores - peak)
    probs = (expo / jnp.sum(expo, axis=-1, keepdims=True)).astype(jnp.bfloat16)
    mixed = jnp.einsum(
        "kgpq,qkd->pkgd", probs, value_rows, preferred_element_type=jnp.float32
    ).reshape(item_count, model_width)
    valid = (place < length).astype(jnp.float32)
    return resid + mixed * valid[:, None]


def body(saved, cot_in, weights, gains, lengths, segments):
    sections = lax.axis_size("pipe")
    n = lax.axis_size("fsdp")
    section = lax.axis_index("pipe")
    carried = cot_in[0, 0]
    model = carried.shape[-1]
    w, g = weights[:, 0], gains[:, 0]
    own_gain = g.astype(jnp.float32)
    kv, cols, gall, w2 = front(n, sections, saved[0, 0], w, own_gain)
    whole_g = jnp.swapaxes(gall, 0, 1).reshape(2, model)
    acc_gain = jnp.zeros((2, model), jnp.float32)
    right = []
    for tick in range(TICKS):
        item = (section + tick) % sections
        layer = item % 2 * sections + item - tick
        active = layer >= 0
        stretch = jnp.maximum(layer, 0) // sections
        length = lengths[item, 0]
        segment = segments[item, 0]
        resid = saved[0, 0, tick].astype(jnp.float32)
        factor = lax.rsqrt(jnp.mean(resid * resid, axis=-1, keepdims=True) + EPS)
        normalized_input, front_pull = jax.vjp(normalize, resid, whole_g[stretch])

        def inner(first, second, third):
            return attend(first, second, third, length, segment)

        _, pull = jax.vjp(inner, resid, normalized_input, kv[tick] * factor)
        direct, normed_cot, keyval_cot = pull(carried.astype(jnp.float32))
        scaled = jnp.where(active, keyval_cot * factor, 0.0).astype(jnp.bfloat16)
        rows_all, product = back(n, sections, tick, scaled, w2)
        right.append(rows_all)
        normed_total = normed_cot + product.astype(jnp.float32) / factor
        resid_cot, gain_cot = front_pull(normed_total)
        acc_gain = acc_gain.at[stretch].add(jnp.where(active, gain_cot, 0.0))
        carried = jnp.where(active, (direct + resid_cot).astype(jnp.bfloat16), carried)
        if tick + 1 < TICKS:
            carried = passed_along(carried, "pipe", -1)
    width = w.shape[1]
    sums = jnp.swapaxes(acc_gain.reshape(2, n, width), 0, 1)
    grad_kv, grad_gain = tail(n, sections, sums, cols, right, own_gain[:, :, None])
    grad_kv = grad_kv[:, None]
    grad_gain = grad_gain.astype(jnp.bfloat16)[:, None]
    return (carried[None, None], grad_kv, grad_gain)


def solution(mesh):
    in_specs = (
        P("pipe", "fsdp", None, None, None),
        P("pipe", "fsdp", None, None),
        P(None, "pipe", "fsdp", None),
        P(None, "pipe", "fsdp"),
        P(None, "fsdp"),
        P(None, "fsdp", None),
    )
    out_specs = (
        P("pipe", "fsdp", None, None),
        P(None, "pipe", "fsdp", None),
        P(None, "pipe", "fsdp"),
    )
    return jax.shard_map(body, mesh=mesh, in_specs=in_specs, out_specs=out_specs, check_vma=False)
```

```python
import functools

import jax
import jax.numpy as jnp
from jax import lax
from jax.experimental import pallas as pl
from jax.experimental.pallas import tpu as pltpu
from jax.sharding import PartitionSpec as P

HEAD_SIZE = 128
KEY_VALUE_HEADS = 4
TICKS = 3
EPS = 1e-05
MESH = pl.DeviceIdType.MESH
LIMIT = 56 * 1024 * 1024


def passed_along(value, axis, by):
    size = lax.axis_size(axis)
    return lax.ppermute(value, axis, [(i, (i + by) % size) for i in range(size)])


def greet_all(n, me):
    barrier = pltpu.get_barrier_semaphore()

    def greet(k, _):
        pl.semaphore_signal(
            barrier, inc=1, device_id={"fsdp": lax.rem(me + k, n)}, device_id_type=MESH
        )
        return 0

    lax.fori_loop(1, n, greet, 0)
    pl.semaphore_wait(barrier, n - 1)


def to_peer(src, dst, send, recv, peer):
    return pltpu.make_async_remote_copy(
        src_ref=src,
        dst_ref=dst,
        send_sem=send,
        recv_sem=recv,
        device_id={"fsdp": peer},
        device_id_type=MESH,
    )


def stretch_of(section, tick, sections):
    item = lax.rem(section + tick, sections)
    layer = lax.rem(item, 2) * sections + item - tick
    return lax.div(jnp.maximum(layer, 0), sections)


def front_kernel(
    n, sections, saved, w, g, kv, cols, gall, w2,
    pair_g, wide, part, ret, xs, xr, fs, fr, ps, pr, gs, gr, ws, wr, qs, qr
):
    me = lax.axis_index("fsdp")
    section = lax.axis_index("pipe")
    width = w.shape[1]
    steps = n // 2
    place, half = lax.div(me, 2), lax.rem(me, 2)
    buddy = place * 2 + 1 - half
    first = stretch_of(section, 0, sections)
    second = 1 - first
    late = stretch_of(section, 2, sections)
    own_rows = pl.ds(pl.multiple_of(half * width, width), width)
    buddy_rows = pl.ds(pl.multiple_of((1 - half) * width, width), width)
    greet_all(n, me)

    def weight_copy(i, stretch):
        return to_peer(w.at[stretch], w2.at[stretch, own_rows], ws.at[i], wr.at[i], buddy)

    def pair_gain_copy():
        return to_peer(g, pair_g.at[half], qs, qr, buddy)

    def column_copy(k, tick):
        to = lax.rem(place + k, steps)
        at = pl.ds(pl.multiple_of(to * 2 * width, 2 * width), 2 * width)
        return to_peer(
            saved.at[tick, :, at], wide.at[k, tick], xs.at[k, tick], xr.at[k, tick],
            to * 2 + half,
        )

    def half_copy(k, tick):
        return to_peer(
            wide.at[k, tick, :, buddy_rows], cols.at[1, k, tick],
            fs.at[k, tick], fr.at[k, tick], buddy,
        )

    def gain_copy(k):
        peer = lax.rem(me + k, n)
        return to_peer(g, gall.at[me], gs.at[k], gr.at[k], peer)

    def back_copy(k, tick):
        to = lax.rem(place - k + steps, steps)
        return to_peer(
            part.at[k, tick], ret.at[k, tick], ps.at[k, tick], pr.at[k, tick],
            to * 2 + half,
        )

    pair_gain_copy().start()
    weight_copy(0, first).start()
    for tick in (0, 2, 1):

        def send(k, _, tick=tick):
            column_copy(k, tick).start()
            return 0

        lax.fori_loop(1, steps, send, 0)
    weight_copy(1, second).start()

    def send_gain(k, _):
        gain_copy(k).start()
        return 0

    lax.fori_loop(1, n, send_gain, 0)
    gall[me] = g[...]
    pair_g[half] = g[...]
    at = pl.ds(pl.multiple_of(place * 2 * width, 2 * width), 2 * width)
    wide[0] = saved[:, :, at]
    w2[:, own_rows, :] = w[...]
    for tick in (0, 2, 1):
        half_copy(0, tick).start()
    pair_gain_copy().wait_recv()

    def share(k, tick):
        stretch = stretch_of(section, tick, sections)
        total = None
        for side in range(2):
            at = pl.ds(side * width, width)
            gain = pair_g[side, pl.ds(stretch, 1), :]
            left = (wide[k, tick, :, at].astype(jnp.float32) * gain).astype(jnp.bfloat16)
            term = jnp.dot(left, w2[stretch, at, :], preferred_element_type=jnp.float32)
            total = term if total is None else total + term
        return total

    weight_copy(0, first).wait_recv()
    for tick in (0, 2, 1):
        if tick == 2:

            @pl.when(late != first)
            def _():
                weight_copy(1, second).wait_recv()

        if tick == 1:

            @pl.when(late == first)
            def _():
                weight_copy(1, second).wait_recv()

        def answer(k, _, tick=tick):
            column_copy(k, tick).wait_recv()
            half_copy(k, tick).start()
            part[k, tick] = share(k, tick).astype(jnp.bfloat16)
            back_copy(k, tick).start()
            return 0

        lax.fori_loop(1, steps, answer, 0)
        kv[tick] = share(0, tick)

    def own_half(k, _):
        cols[0, k] = wide[k, :, :, own_rows]
        return 0

    lax.fori_loop(0, steps, own_half, 0)
    for tick in (0, 2, 1):

        def collect(k, _, tick=tick):
            back_copy(k, tick).wait_recv()
            kv[tick] += ret[k, tick].astype(jnp.float32)
            return 0

        lax.fori_loop(1, steps, collect, 0)
        half_copy(0, tick).wait()

        def finish(k, _, tick=tick):
            column_copy(k, tick).wait_send()
            half_copy(k, tick).wait()
            back_copy(k, tick).wait_send()
            return 0

        lax.fori_loop(1, steps, finish, 0)

    def finish_gain(k, _):
        gain_copy(k).wait()
        return 0

    lax.fori_loop(1, n, finish_gain, 0)
    pair_gain_copy().wait_send()
    weight_copy(0, first).wait_send()
    weight_copy(1, second).wait_send()


def front(n, sections, saved, w, g):
    ticks, rows, model = saved.shape
    width, kvw = w.shape[1:]
    steps = n // 2
    vmem = pl.BlockSpec(memory_space=pltpu.VMEM)
    dma = pltpu.SemaphoreType.DMA
    return pl.pallas_call(
        functools.partial(front_kernel, n, sections),
        out_shape=(
            jax.ShapeDtypeStruct((ticks, rows, kvw), jnp.float32),
            jax.ShapeDtypeStruct((2, steps, ticks, rows, width), jnp.bfloat16),
            jax.ShapeDtypeStruct((n, 2, width), jnp.float32),
            jax.ShapeDtypeStruct((2, 2 * width, kvw), jnp.bfloat16),
        ),
        in_specs=[vmem] * 3,
        out_specs=(vmem,) * 4,
        scratch_shapes=[
            pltpu.VMEM((2, 2, width), jnp.float32),
            pltpu.VMEM((steps, ticks, rows, 2 * width), jnp.bfloat16),
            pltpu.VMEM((steps, ticks, rows, kvw), jnp.bfloat16),
            pltpu.VMEM((steps, ticks, rows, kvw), jnp.bfloat16),
        ]
        + [dma((steps, ticks))] * 6
        + [dma((n,))] * 2
        + [dma((2,))] * 2
        + [dma] * 2,
        compiler_params=pltpu.CompilerParams(
            collective_id=0, has_side_effects=True, vmem_limit_bytes=LIMIT
        ),
    )(saved, w, g)


def back_kernel(
    n, sections, tick, kc, w2, rows_all, total, part, ks, kr, fs, fr, ps, pr
):
    me = lax.axis_index("fsdp")
    section = lax.axis_index("pipe")
    wide = w2.shape[1]
    steps = n // 2
    place, half = lax.div(me, 2), lax.rem(me, 2)
    buddy = place * 2 + 1 - half
    stretch = stretch_of(section, tick, sections)
    mine = pl.ds(pl.multiple_of(place * wide, wide), wide)
    greet_all(n, me)

    def row_copy(k):
        to = lax.rem(place + k, steps) * 2 + half
        return to_peer(kc, rows_all.at[0, k], ks.at[k], kr.at[k], to)

    def own_copy():
        return to_peer(kc, rows_all.at[1, 0], fs.at[0], fr.at[0], buddy)

    def pair_copy(k):
        return to_peer(rows_all.at[0, k], rows_all.at[1, k], fs.at[k], fr.at[k], buddy)

    def back_copy(k):
        to = lax.rem(place - k + steps, steps) * 2 + half
        return to_peer(part.at[k], total.at[:, mine], ps.at[k], pr.at[k], to)

    def send(k, _):
        row_copy(k).start()
        return 0

    lax.fori_loop(1, steps, send, 0)
    own_copy().start()
    rows_all[0, 0] = kc[...]

    def share(k):
        return lax.dot_general(
            rows_all[0, k], w2[stretch], (((1,), (1,)), ((), ())),
            preferred_element_type=jnp.float32,
        ).astype(jnp.bfloat16)

    total[:, mine] = share(0)

    def answer(k, _):
        row_copy(k).wait_recv()
        pair_copy(k).start()
        part[k] = share(k)
        back_copy(k).start()
        return 0

    lax.fori_loop(1, steps, answer, 0)
    own_copy().wait()

    def finish(k, _):
        row_copy(k).wait_send()
        pair_copy(k).wait()
        back_copy(k).wait()
        return 0

    lax.fori_loop(1, steps, finish, 0)


def back(n, sections, tick, kc, w2):
    rows, kvw = kc.shape
    wide = w2.shape[1]
    steps = n // 2
    vmem = pl.BlockSpec(memory_space=pltpu.VMEM)
    return pl.pallas_call(
        functools.partial(back_kernel, n, sections, tick),
        out_shape=(
            jax.ShapeDtypeStruct((2, steps, rows, kvw), jnp.bfloat16),
            jax.ShapeDtypeStruct((rows, steps * wide), jnp.bfloat16),
        ),
        in_specs=[vmem] * 2,
        out_specs=(vmem,) * 2,
        scratch_shapes=[pltpu.VMEM((steps, rows, wide), jnp.bfloat16)]
        + [pltpu.SemaphoreType.DMA((steps,))] * 6,
        compiler_params=pltpu.CompilerParams(
            collective_id=1 + tick, has_side_effects=True, vmem_limit_bytes=LIMIT
        ),
    )(kc, w2)


def tail_kernel(
    n, sections, sums, cols, first, second, third, g, grad, gain, got, acc, ss, sr
):
    me = lax.axis_index("fsdp")
    section = lax.axis_index("pipe")
    greet_all(n, me)

    def copy(k):
        peer = lax.rem(me + k, n)
        return to_peer(sums.at[peer], got.at[k], ss.at[k], sr.at[k], peer)

    def send(k, _):
        copy(k).start()
        return 0

    lax.fori_loop(1, n, send, 0)
    acc[...] = jnp.zeros_like(acc)
    for tick, rows in enumerate((first, second, third)):
        stretch = stretch_of(section, tick, sections)
        left = cols[:, :, tick].reshape(-1, cols.shape[-1])
        right = rows[...].reshape(left.shape[0], -1)
        acc[stretch] += lax.dot_general(
            left, right, (((0,), (0,)), ((), ())), preferred_element_type=jnp.float32
        )
    grad[...] = (acc[...] * g[...]).astype(jnp.bfloat16)
    gain[...] = sums[me]

    def collect(k, _):
        copy(k).wait()
        gain[...] += got[k]
        return 0

    lax.fori_loop(1, n, collect, 0)


def tail(n, sections, sums, cols, rows, g):
    kvw = rows[0].shape[-1]
    vmem = pl.BlockSpec(memory_space=pltpu.VMEM)
    return pl.pallas_call(
        functools.partial(tail_kernel, n, sections),
        out_shape=(
            jax.ShapeDtypeStruct((2, cols.shape[-1], kvw), jnp.bfloat16),
            jax.ShapeDtypeStruct(sums.shape[1:], jnp.float32),
        ),
        in_specs=[vmem] * 6,
        out_specs=(vmem,) * 2,
        scratch_shapes=[
            pltpu.VMEM(sums.shape, jnp.float32),
            pltpu.VMEM((2, cols.shape[-1], kvw), jnp.float32),
        ]
        + [pltpu.SemaphoreType.DMA((n,))] * 2,
        compiler_params=pltpu.CompilerParams(
            collective_id=1 + TICKS, has_side_effects=True, vmem_limit_bytes=LIMIT
        ),
    )(sums, cols, *rows, g)


def normalize(resid, gain):
    factor = lax.rsqrt(jnp.mean(resid * resid, axis=-1, keepdims=True) + EPS)
    return resid * factor * gain


def attend_kernel(x, gain, raw, cot, allowed, valid, kc, ncot):
    rows, model = x.shape
    groups = model // HEAD_SIZE // KEY_VALUE_HEADS
    half = KEY_VALUE_HEADS * HEAD_SIZE
    resid = x[...].astype(jnp.float32)
    factor = lax.rsqrt(jnp.mean(resid * resid, axis=-1, keepdims=True) + EPS)
    normed = (resid * factor * gain[...]).astype(jnp.bfloat16)
    mixed_cot = (cot[...].astype(jnp.float32) * valid[...]).astype(jnp.bfloat16)
    seen = jnp.concatenate([allowed[...]] * groups, axis=0) > 0.5
    across = (((1,), (1,)), ((), ()))
    down = (((0,), (0,)), ((), ()))

    def heads(value, at):
        first = at * groups
        return jnp.concatenate(
            [
                value[:, (first + i) * HEAD_SIZE : (first + i + 1) * HEAD_SIZE]
                for i in range(groups)
            ],
            axis=0,
        )

    for at in range(KEY_VALUE_HEADS):
        key_at = slice(at * HEAD_SIZE, (at + 1) * HEAD_SIZE)
        value_at = slice(half + at * HEAD_SIZE, half + (at + 1) * HEAD_SIZE)
        keys = (raw[:, key_at] * factor).astype(jnp.bfloat16)
        values = (raw[:, value_at] * factor).astype(jnp.bfloat16)
        query = heads(normed, at)
        pulled = heads(mixed_cot, at)
        scores = lax.dot_general(query, keys, across, preferred_element_type=jnp.float32)
        scores = jnp.where(seen, scores * HEAD_SIZE ** (-0.5), -1e30)
        expo = jnp.exp(scores - jnp.max(scores, axis=-1, keepdims=True))
        probs = expo / jnp.sum(expo, axis=-1, keepdims=True)
        prob_cot = lax.dot_general(
            pulled, values, across, preferred_element_type=jnp.float32
        )
        prob_cot = prob_cot.astype(jnp.bfloat16).astype(jnp.float32)
        inner = jnp.sum(probs * prob_cot, axis=-1, keepdims=True)
        score_cot = jnp.where(seen, probs * (prob_cot - inner), 0.0) * HEAD_SIZE ** (-0.5)
        score_cot = score_cot.astype(jnp.bfloat16)
        query_cot = jnp.dot(score_cot, keys, preferred_element_type=jnp.float32)
        for i in range(groups):
            head = at * groups + i
            ncot[:, head * HEAD_SIZE : (head + 1) * HEAD_SIZE] = query_cot[
                i * rows : (i + 1) * rows
            ].astype(jnp.bfloat16)
        key_cot = lax.dot_general(score_cot, query, down, preferred_element_type=jnp.float32)
        value_cot = lax.dot_general(
            probs.astype(jnp.bfloat16), pulled, down, preferred_element_type=jnp.float32
        )
        kc[:, key_at] = (key_cot * factor).astype(jnp.bfloat16)
        kc[:, value_at] = (value_cot * factor).astype(jnp.bfloat16)


def attend_back(x, gain, raw, cot, allowed, valid):
    vmem = pl.BlockSpec(memory_space=pltpu.VMEM)
    return pl.pallas_call(
        attend_kernel,
        out_shape=(
            jax.ShapeDtypeStruct(raw.shape, jnp.bfloat16),
            jax.ShapeDtypeStruct(x.shape, jnp.bfloat16),
        ),
        in_specs=[vmem] * 6,
        out_specs=(vmem,) * 2,
        cost_estimate=pl.CostEstimate(
            flops=500_000_000, bytes_accessed=3_000_000, transcendentals=200_000
        ),
        compiler_params=pltpu.CompilerParams(vmem_limit_bytes=LIMIT),
    )(x, gain, raw, cot, allowed, valid)


def body(saved, cot_in, weights, gains, lengths, segments):
    sections = lax.axis_size("pipe")
    n = lax.axis_size("fsdp")
    section = lax.axis_index("pipe")
    carried = cot_in[0, 0]
    model = carried.shape[-1]
    w, g = weights[:, 0], gains[:, 0]
    own_gain = g.astype(jnp.float32)
    kv, cols, gall, w2 = front(n, sections, saved[0, 0], w, own_gain)
    whole_g = jnp.swapaxes(gall, 0, 1).reshape(2, model)
    acc_gain = jnp.zeros((2, model), jnp.float32)
    right = []
    for tick in range(TICKS):
        item = (section + tick) % sections
        layer = item % 2 * sections + item - tick
        active = layer >= 0
        stretch = jnp.maximum(layer, 0) // sections
        length = lengths[item, 0]
        segment = segments[item, 0]
        resid = saved[0, 0, tick].astype(jnp.float32)
        factor = lax.rsqrt(jnp.mean(resid * resid, axis=-1, keepdims=True) + EPS)
        _, front_pull = jax.vjp(normalize, resid, whole_g[stretch])
        place = jnp.arange(resid.shape[0], dtype=jnp.int32)
        allowed = (
            (segment[:, None] == segment[None, :])
            & (place[None, :] <= place[:, None])
            & (place[None, :] < length)
        )
        allowed = (allowed | (place[:, None] == place[None, :])).astype(jnp.float32)
        valid = ((place < length) & active).astype(jnp.float32)[:, None]
        scaled, normed_cot = attend_back(
            saved[0, 0, tick], whole_g[stretch][None], kv[tick], carried, allowed, valid
        )
        rows_all, product = back(n, sections, tick, scaled, w2)
        right.append(rows_all)
        normed_total = normed_cot.astype(jnp.float32) + product.astype(jnp.float32) / factor
        resid_cot, gain_cot = front_pull(normed_total)
        acc_gain = acc_gain.at[stretch].add(jnp.where(active, gain_cot, 0.0))
        carried = jnp.where(active, (carried.astype(jnp.float32) + resid_cot).astype(jnp.bfloat16), carried)
        if tick + 1 < TICKS:
            carried = passed_along(carried, "pipe", -1)
    width = w.shape[1]
    sums = jnp.swapaxes(acc_gain.reshape(2, n, width), 0, 1)
    grad_kv, grad_gain = tail(n, sections, sums, cols, right, own_gain[:, :, None])
    grad_kv = grad_kv[:, None]
    grad_gain = grad_gain.astype(jnp.bfloat16)[:, None]
    return (carried[None, None], grad_kv, grad_gain)


def solution(mesh):
    in_specs = (
        P("pipe", "fsdp", None, None, None),
        P("pipe", "fsdp", None, None),
        P(None, "pipe", "fsdp", None),
        P(None, "pipe", "fsdp"),
        P(None, "fsdp"),
        P(None, "fsdp", None),
    )
    out_specs = (
        P("pipe", "fsdp", None, None),
        P(None, "pipe", "fsdp", None),
        P(None, "pipe", "fsdp"),
    )
    return jax.shard_map(body, mesh=mesh, in_specs=in_specs, out_specs=out_specs, check_vma=False)
```

```python
import functools

import jax
import jax.numpy as jnp
from jax import lax
from jax.experimental import pallas as pl
from jax.experimental.pallas import tpu as pltpu
from jax.sharding import PartitionSpec as P

HEAD_SIZE = 128
KEY_VALUE_HEADS = 4
TICKS = 3
EPS = 1e-05
MESH = pl.DeviceIdType.MESH
LIMIT = 56 * 1024 * 1024


def passed_along(value, axis, by):
    size = lax.axis_size(axis)
    return lax.ppermute(value, axis, [(i, (i + by) % size) for i in range(size)])


def greet_all(n, me):
    barrier = pltpu.get_barrier_semaphore()

    def greet(k, _):
        pl.semaphore_signal(
            barrier, inc=1, device_id={"fsdp": lax.rem(me + k, n)}, device_id_type=MESH
        )
        return 0

    lax.fori_loop(1, n, greet, 0)
    pl.semaphore_wait(barrier, n - 1)


def to_peer(src, dst, send, recv, peer):
    return pltpu.make_async_remote_copy(
        src_ref=src,
        dst_ref=dst,
        send_sem=send,
        recv_sem=recv,
        device_id={"fsdp": peer},
        device_id_type=MESH,
    )


def stretch_of(section, tick, sections):
    item = lax.rem(section + tick, sections)
    layer = lax.rem(item, 2) * sections + item - tick
    return lax.div(jnp.maximum(layer, 0), sections)


def front_kernel(
    n, sections, saved, w, g, kv, cols, gall, w2,
    pair_g, wide, part, ret, xs, xr, fs, fr, ps, pr, gs, gr, ws, wr, qs, qr
):
    me = lax.axis_index("fsdp")
    section = lax.axis_index("pipe")
    width = w.shape[1]
    steps = n // 2
    place, half = lax.div(me, 2), lax.rem(me, 2)
    buddy = place * 2 + 1 - half
    first = stretch_of(section, 0, sections)
    second = 1 - first
    late = stretch_of(section, 2, sections)
    own_rows = pl.ds(pl.multiple_of(half * width, width), width)
    buddy_rows = pl.ds(pl.multiple_of((1 - half) * width, width), width)
    greet_all(n, me)

    def weight_copy(i, stretch):
        return to_peer(w.at[stretch], w2.at[stretch, own_rows], ws.at[i], wr.at[i], buddy)

    def pair_gain_copy():
        return to_peer(g, pair_g.at[half], qs, qr, buddy)

    def column_copy(k, tick):
        to = lax.rem(place + k, steps)
        at = pl.ds(pl.multiple_of(to * 2 * width, 2 * width), 2 * width)
        return to_peer(
            saved.at[tick, :, at], wide.at[k, tick], xs.at[k, tick], xr.at[k, tick],
            to * 2 + half,
        )

    def half_copy(k, tick):
        return to_peer(
            wide.at[k, tick, :, buddy_rows], cols.at[1, k, tick],
            fs.at[k, tick], fr.at[k, tick], buddy,
        )

    def gain_copy(k):
        peer = lax.rem(me + k, n)
        return to_peer(g, gall.at[me], gs.at[k], gr.at[k], peer)

    def back_copy(k, tick):
        to = lax.rem(place - k + steps, steps)
        return to_peer(
            part.at[k, tick], ret.at[k, tick], ps.at[k, tick], pr.at[k, tick],
            to * 2 + half,
        )

    pair_gain_copy().start()
    weight_copy(0, first).start()
    for tick in (0, 2, 1):

        def send(k, _, tick=tick):
            column_copy(k, tick).start()
            return 0

        lax.fori_loop(1, steps, send, 0)
    weight_copy(1, second).start()

    def send_gain(k, _):
        gain_copy(k).start()
        return 0

    lax.fori_loop(1, n, send_gain, 0)
    gall[me] = g[...]
    pair_g[half] = g[...]
    at = pl.ds(pl.multiple_of(place * 2 * width, 2 * width), 2 * width)
    wide[0] = saved[:, :, at]
    w2[:, own_rows, :] = w[...]
    for tick in (0, 2, 1):
        half_copy(0, tick).start()
    pair_gain_copy().wait_recv()

    def share(k, tick):
        stretch = stretch_of(section, tick, sections)
        total = None
        for side in range(2):
            at = pl.ds(side * width, width)
            gain = pair_g[side, pl.ds(stretch, 1), :]
            left = (wide[k, tick, :, at].astype(jnp.float32) * gain).astype(jnp.bfloat16)
            term = jnp.dot(left, w2[stretch, at, :], preferred_element_type=jnp.float32)
            total = term if total is None else total + term
        return total

    weight_copy(0, first).wait_recv()
    for tick in (0, 2, 1):
        if tick == 2:

            @pl.when(late != first)
            def _():
                weight_copy(1, second).wait_recv()

        if tick == 1:

            @pl.when(late == first)
            def _():
                weight_copy(1, second).wait_recv()

        def answer(k, _, tick=tick):
            column_copy(k, tick).wait_recv()
            half_copy(k, tick).start()
            part[k, tick] = share(k, tick).astype(jnp.bfloat16)
            back_copy(k, tick).start()
            return 0

        lax.fori_loop(1, steps, answer, 0)
        kv[tick] = share(0, tick)

    def own_half(k, _):
        cols[0, k] = wide[k, :, :, own_rows]
        return 0

    lax.fori_loop(0, steps, own_half, 0)
    for tick in (0, 2, 1):

        def collect(k, _, tick=tick):
            back_copy(k, tick).wait_recv()
            kv[tick] += ret[k, tick].astype(jnp.float32)
            return 0

        lax.fori_loop(1, steps, collect, 0)
        half_copy(0, tick).wait()

        def finish(k, _, tick=tick):
            column_copy(k, tick).wait_send()
            half_copy(k, tick).wait()
            back_copy(k, tick).wait_send()
            return 0

        lax.fori_loop(1, steps, finish, 0)

    def finish_gain(k, _):
        gain_copy(k).wait()
        return 0

    lax.fori_loop(1, n, finish_gain, 0)
    pair_gain_copy().wait_send()
    weight_copy(0, first).wait_send()
    weight_copy(1, second).wait_send()


def front(n, sections, saved, w, g):
    ticks, rows, model = saved.shape
    width, kvw = w.shape[1:]
    steps = n // 2
    vmem = pl.BlockSpec(memory_space=pltpu.VMEM)
    dma = pltpu.SemaphoreType.DMA
    return pl.pallas_call(
        functools.partial(front_kernel, n, sections),
        out_shape=(
            jax.ShapeDtypeStruct((ticks, rows, kvw), jnp.float32),
            jax.ShapeDtypeStruct((2, steps, ticks, rows, width), jnp.bfloat16),
            jax.ShapeDtypeStruct((n, 2, width), jnp.float32),
            jax.ShapeDtypeStruct((2, 2 * width, kvw), jnp.bfloat16),
        ),
        in_specs=[vmem] * 3,
        out_specs=(vmem,) * 4,
        scratch_shapes=[
            pltpu.VMEM((2, 2, width), jnp.float32),
            pltpu.VMEM((steps, ticks, rows, 2 * width), jnp.bfloat16),
            pltpu.VMEM((steps, ticks, rows, kvw), jnp.bfloat16),
            pltpu.VMEM((steps, ticks, rows, kvw), jnp.bfloat16),
        ]
        + [dma((steps, ticks))] * 6
        + [dma((n,))] * 2
        + [dma((2,))] * 2
        + [dma] * 2,
        compiler_params=pltpu.CompilerParams(
            collective_id=0, has_side_effects=True, vmem_limit_bytes=LIMIT
        ),
    )(saved, w, g)


def back_kernel(
    n, sections, tick, kc, w2, rows_all, total, part, ks, kr, ls, fs, fr, ps, pr
):
    me = lax.axis_index("fsdp")
    section = lax.axis_index("pipe")
    wide = w2.shape[1]
    steps = n // 2
    place, half = lax.div(me, 2), lax.rem(me, 2)
    buddy = place * 2 + 1 - half
    stretch = stretch_of(section, tick, sections)
    mine = pl.ds(pl.multiple_of(place * wide, wide), wide)
    greet_all(n, me)

    def right(d):
        to = lax.rem(place + 1, steps) * 2 + half
        return to_peer(
            rows_all.at[0, d], rows_all.at[0, d + 1], ks.at[d], kr.at[d + 1], to
        )

    def left(d):
        to = lax.rem(place + steps - 1, steps) * 2 + half
        slot = steps - d - 1
        return to_peer(
            rows_all.at[0, lax.rem(steps - d, steps)], rows_all.at[0, slot],
            ls.at[d], kr.at[slot], to,
        )

    def own_copy():
        return to_peer(kc, rows_all.at[1, 0], fs.at[0], fr.at[0], buddy)

    def pair_copy(k):
        return to_peer(rows_all.at[0, k], rows_all.at[1, k], fs.at[k], fr.at[k], buddy)

    def back_copy(k):
        to = lax.rem(place - k + steps, steps) * 2 + half
        return to_peer(part.at[k], total.at[:, mine], ps.at[k], pr.at[k], to)

    rows_all[0, 0] = kc[...]
    has_right, has_left = place + 1 < steps, place >= 1

    @pl.when(has_right)
    def _():
        right(0).start()

    @pl.when(has_left)
    def _():
        left(0).start()

    own_copy().start()

    def share(k):
        return lax.dot_general(
            rows_all[0, k], w2[stretch], (((1,), (1,)), ((), ())),
            preferred_element_type=jnp.float32,
        ).astype(jnp.bfloat16)

    total[:, mine] = share(0)

    def handle(k):
        pair_copy(k).start()
        part[k] = share(k)
        back_copy(k).start()

    def answer(d, _):
        @pl.when(place >= d)
        def _():
            right(d - 1).wait_recv()

            @pl.when(has_right)
            def _():
                right(d).start()

            handle(d)

        @pl.when(place + d < steps)
        def _():
            left(d - 1).wait_recv()

            @pl.when(has_left)
            def _():
                left(d).start()

            handle(steps - d)

        return 0

    lax.fori_loop(1, steps, answer, 0)
    own_copy().wait()

    def finish(k, _):
        pair_copy(k).wait()
        back_copy(k).wait()

        @pl.when((place >= k - 1) & has_right)
        def _():
            right(k - 1).wait_send()

        @pl.when((place + k - 1 < steps) & has_left)
        def _():
            left(k - 1).wait_send()

        return 0

    lax.fori_loop(1, steps, finish, 0)


def back(n, sections, tick, kc, w2):
    rows, kvw = kc.shape
    wide = w2.shape[1]
    steps = n // 2
    vmem = pl.BlockSpec(memory_space=pltpu.VMEM)
    return pl.pallas_call(
        functools.partial(back_kernel, n, sections, tick),
        out_shape=(
            jax.ShapeDtypeStruct((2, steps, rows, kvw), jnp.bfloat16),
            jax.ShapeDtypeStruct((rows, steps * wide), jnp.bfloat16),
        ),
        in_specs=[vmem] * 2,
        out_specs=(vmem,) * 2,
        scratch_shapes=[pltpu.VMEM((steps, rows, wide), jnp.bfloat16)]
        + [pltpu.SemaphoreType.DMA((steps,))] * 7,
        compiler_params=pltpu.CompilerParams(
            collective_id=1 + tick, has_side_effects=True, vmem_limit_bytes=LIMIT
        ),
    )(kc, w2)


def tail_kernel(
    n, sections, sums, cols, first, second, third, g, grad, gain, got, acc, ss, sr
):
    me = lax.axis_index("fsdp")
    section = lax.axis_index("pipe")
    greet_all(n, me)

    def copy(k):
        peer = lax.rem(me + k, n)
        return to_peer(sums.at[peer], got.at[k], ss.at[k], sr.at[k], peer)

    def send(k, _):
        copy(k).start()
        return 0

    lax.fori_loop(1, n, send, 0)
    acc[...] = jnp.zeros_like(acc)
    for tick, rows in enumerate((first, second, third)):
        stretch = stretch_of(section, tick, sections)
        left = cols[:, :, tick].reshape(-1, cols.shape[-1])
        right = rows[...].reshape(left.shape[0], -1)
        acc[stretch] += lax.dot_general(
            left, right, (((0,), (0,)), ((), ())), preferred_element_type=jnp.float32
        )
    grad[...] = (acc[...] * g[...]).astype(jnp.bfloat16)
    gain[...] = sums[me]

    def collect(k, _):
        copy(k).wait()
        gain[...] += got[k]
        return 0

    lax.fori_loop(1, n, collect, 0)


def tail(n, sections, sums, cols, rows, g):
    kvw = rows[0].shape[-1]
    vmem = pl.BlockSpec(memory_space=pltpu.VMEM)
    return pl.pallas_call(
        functools.partial(tail_kernel, n, sections),
        out_shape=(
            jax.ShapeDtypeStruct((2, cols.shape[-1], kvw), jnp.bfloat16),
            jax.ShapeDtypeStruct(sums.shape[1:], jnp.float32),
        ),
        in_specs=[vmem] * 6,
        out_specs=(vmem,) * 2,
        scratch_shapes=[
            pltpu.VMEM(sums.shape, jnp.float32),
            pltpu.VMEM((2, cols.shape[-1], kvw), jnp.float32),
        ]
        + [pltpu.SemaphoreType.DMA((n,))] * 2,
        compiler_params=pltpu.CompilerParams(
            collective_id=1 + TICKS, has_side_effects=True, vmem_limit_bytes=LIMIT
        ),
    )(sums, cols, *rows, g)


def normalize(resid, gain):
    factor = lax.rsqrt(jnp.mean(resid * resid, axis=-1, keepdims=True) + EPS)
    return resid * factor * gain


def attend_kernel(x, gain, raw, cot, allowed, valid, kc, ncot):
    rows, model = x.shape
    groups = model // HEAD_SIZE // KEY_VALUE_HEADS
    half = KEY_VALUE_HEADS * HEAD_SIZE
    resid = x[...].astype(jnp.float32)
    factor = lax.rsqrt(jnp.mean(resid * resid, axis=-1, keepdims=True) + EPS)
    normed = (resid * factor * gain[...]).astype(jnp.bfloat16)
    mixed_cot = (cot[...].astype(jnp.float32) * valid[...]).astype(jnp.bfloat16)
    seen = jnp.concatenate([allowed[...]] * groups, axis=0) > 0.5
    across = (((1,), (1,)), ((), ()))
    down = (((0,), (0,)), ((), ()))

    def heads(value, at):
        first = at * groups
        return jnp.concatenate(
            [
                value[:, (first + i) * HEAD_SIZE : (first + i + 1) * HEAD_SIZE]
                for i in range(groups)
            ],
            axis=0,
        )

    for at in range(KEY_VALUE_HEADS):
        key_at = slice(at * HEAD_SIZE, (at + 1) * HEAD_SIZE)
        value_at = slice(half + at * HEAD_SIZE, half + (at + 1) * HEAD_SIZE)
        keys = (raw[:, key_at] * factor).astype(jnp.bfloat16)
        values = (raw[:, value_at] * factor).astype(jnp.bfloat16)
        query = heads(normed, at)
        pulled = heads(mixed_cot, at)
        scores = lax.dot_general(query, keys, across, preferred_element_type=jnp.float32)
        scores = jnp.where(seen, scores * HEAD_SIZE ** (-0.5), -1e30)
        expo = jnp.exp(scores - jnp.max(scores, axis=-1, keepdims=True))
        probs = expo / jnp.sum(expo, axis=-1, keepdims=True)
        prob_cot = lax.dot_general(
            pulled, values, across, preferred_element_type=jnp.float32
        )
        prob_cot = prob_cot.astype(jnp.bfloat16).astype(jnp.float32)
        inner = jnp.sum(probs * prob_cot, axis=-1, keepdims=True)
        score_cot = jnp.where(seen, probs * (prob_cot - inner), 0.0) * HEAD_SIZE ** (-0.5)
        score_cot = score_cot.astype(jnp.bfloat16)
        query_cot = jnp.dot(score_cot, keys, preferred_element_type=jnp.float32)
        for i in range(groups):
            head = at * groups + i
            ncot[:, head * HEAD_SIZE : (head + 1) * HEAD_SIZE] = query_cot[
                i * rows : (i + 1) * rows
            ].astype(jnp.bfloat16)
        key_cot = lax.dot_general(score_cot, query, down, preferred_element_type=jnp.float32)
        value_cot = lax.dot_general(
            probs.astype(jnp.bfloat16), pulled, down, preferred_element_type=jnp.float32
        )
        kc[:, key_at] = (key_cot * factor).astype(jnp.bfloat16)
        kc[:, value_at] = (value_cot * factor).astype(jnp.bfloat16)


def attend_back(x, gain, raw, cot, allowed, valid):
    vmem = pl.BlockSpec(memory_space=pltpu.VMEM)
    return pl.pallas_call(
        attend_kernel,
        out_shape=(
            jax.ShapeDtypeStruct(raw.shape, jnp.bfloat16),
            jax.ShapeDtypeStruct(x.shape, jnp.bfloat16),
        ),
        in_specs=[vmem] * 6,
        out_specs=(vmem,) * 2,
        cost_estimate=pl.CostEstimate(
            flops=500_000_000, bytes_accessed=3_000_000, transcendentals=200_000
        ),
        compiler_params=pltpu.CompilerParams(vmem_limit_bytes=LIMIT),
    )(x, gain, raw, cot, allowed, valid)


def body(saved, cot_in, weights, gains, lengths, segments):
    sections = lax.axis_size("pipe")
    n = lax.axis_size("fsdp")
    section = lax.axis_index("pipe")
    carried = cot_in[0, 0]
    model = carried.shape[-1]
    w, g = weights[:, 0], gains[:, 0]
    own_gain = g.astype(jnp.float32)
    kv, cols, gall, w2 = front(n, sections, saved[0, 0], w, own_gain)
    whole_g = jnp.swapaxes(gall, 0, 1).reshape(2, model)
    acc_gain = jnp.zeros((2, model), jnp.float32)
    right = []
    for tick in range(TICKS):
        item = (section + tick) % sections
        layer = item % 2 * sections + item - tick
        active = layer >= 0
        stretch = jnp.maximum(layer, 0) // sections
        length = lengths[item, 0]
        segment = segments[item, 0]
        resid = saved[0, 0, tick].astype(jnp.float32)
        factor = lax.rsqrt(jnp.mean(resid * resid, axis=-1, keepdims=True) + EPS)
        _, front_pull = jax.vjp(normalize, resid, whole_g[stretch])
        place = jnp.arange(resid.shape[0], dtype=jnp.int32)
        allowed = (
            (segment[:, None] == segment[None, :])
            & (place[None, :] <= place[:, None])
            & (place[None, :] < length)
        )
        allowed = (allowed | (place[:, None] == place[None, :])).astype(jnp.float32)
        valid = ((place < length) & active).astype(jnp.float32)[:, None]
        scaled, normed_cot = attend_back(
            saved[0, 0, tick], whole_g[stretch][None], kv[tick], carried, allowed, valid
        )
        rows_all, product = back(n, sections, tick, scaled, w2)
        right.append(rows_all)
        normed_total = normed_cot.astype(jnp.float32) + product.astype(jnp.float32) / factor
        resid_cot, gain_cot = front_pull(normed_total)
        acc_gain = acc_gain.at[stretch].add(jnp.where(active, gain_cot, 0.0))
        carried = jnp.where(active, (carried.astype(jnp.float32) + resid_cot).astype(jnp.bfloat16), carried)
        if tick + 1 < TICKS:
            carried = passed_along(carried, "pipe", -1)
    width = w.shape[1]
    sums = jnp.swapaxes(acc_gain.reshape(2, n, width), 0, 1)
    grad_kv, grad_gain = tail(n, sections, sums, cols, right, own_gain[:, :, None])
    grad_kv = grad_kv[:, None]
    grad_gain = grad_gain.astype(jnp.bfloat16)[:, None]
    return (carried[None, None], grad_kv, grad_gain)


def solution(mesh):
    in_specs = (
        P("pipe", "fsdp", None, None, None),
        P("pipe", "fsdp", None, None),
        P(None, "pipe", "fsdp", None),
        P(None, "pipe", "fsdp"),
        P(None, "fsdp"),
        P(None, "fsdp", None),
    )
    out_specs = (
        P("pipe", "fsdp", None, None),
        P(None, "pipe", "fsdp", None),
        P(None, "pipe", "fsdp"),
    )
    return jax.shard_map(body, mesh=mesh, in_specs=in_specs, out_specs=out_specs, check_vma=False)
```
